32 devices in a mesh: gx: 4 (over y, x), gy: 4 (over z), gz: 2 (over core).
Axes of the slice: x: 2, y: 2, z: 4, core: 2. Of those that a mesh axis runs over, the one named last changes fastest.
Arguments:
- fields: float32 [24, 32, 128, 256], P(None, 'gx', 'gy', 'gz'), may hold values from -8.5 to 8.5
- velocity: float32 [3, 32, 128, 256], P(None, 'gx', 'gy', 'gz'), may hold values from -0.4 to 0.4
- diffusivity: float32 [24], replicated, may hold values from 0.02 to 0.15
- weight_in: bfloat16 [24, 1600], replicated, may hold values from -1.25 to 1.25
- bias_in: float32 [1600], replicated, may hold values from -3 to 3
- weight_mid: bfloat16 [1600, 800], replicated, may hold values from -0.15625 to 0.15625
- bias_mid: float32 [800], replicated, may hold values from -3 to 3
- weight_low: bfloat16 [800, 400], replicated, may hold values from -0.21875 to 0.21875
- bias_low: float32 [400], replicated, may hold values from -3 to 3
- weight_out: bfloat16 [400, 24], replicated, may hold values from -0.3125 to 0.3125
- bias_out: float32 [24], replicated, may hold values from -3 to 3
- react_list: int32 [32, 96], P(('gx', 'gy', 'gz')), may hold values from -1 to 255, as said below
- owner_table: int32 [32, 96], P(('gx', 'gy', 'gz')), may hold values from -1 to 31, as said below
Outputs:
- updated: float32 [24, 32, 128, 256], P(None, 'gx', 'gy', 'gz')
- owner_activity: float32 [32], P(('gx', 'gy', 'gz'))
The draws below stay inside these ranges and needn't reach their ends.
Inputs may be any that keep to these rules, and one draw needn't show every extreme that they name: `react_list`: row d lists distinct blocks of brick d, valid entries first and -1 after them; a brick lists at most 96 blocks and some brick lists exactly 96; all bricks together list 32 times the number of devices. owner_table[d, i] is -1 exactly where react_list[d, i] is, else the owner's index over gx+gy+gz; every device owns exactly 32 blocks; no brick sends more than 3 blocks to one owner, and some brick sends exactly 3 to some owner.
All inputs are finite; a program needn't handle non-finite values.
Results may differ from the reference program's by a relative error of at most 0.00058.
Values may be sent and summed in bfloat16 or wider, within the bound.
A program may use at most 256 MiB of HBM per device.

```python
import math
import jax
import jax.numpy as jnp
from jax import lax

FIELDS = 24
HID_ONE = 1600
HID_TWO = 800
HID_THREE = 400
CX = 8
CY = 32
CZ = 128
OWNED = 32
LIST_MAX = 96
NX = 32
NY = 128
NZ = 256
N_GX = 4
N_GY = 4
N_GZ = 2
DEVICES = 32


def draw_fields(key, part):
    base_key = jax.random.fold_in(key, 11)
    key_scale, key_values = jax.random.split(base_key, 2)
    column_scale = jnp.exp(jax.random.uniform(key_scale, (FIELDS, NX, NY, 1), jnp.float32, jnp.log(0.5), jnp.log(2.0)))
    rough = jnp.clip(jax.random.normal(key_values, (FIELDS, NX, NY, NZ), jnp.float32), -4.0, 4.0)
    return (rough * column_scale).astype(jnp.float32)


def layout(key):
    base_key = jax.random.fold_in(key, 5)
    key_first, key_second, key_place, key_blocks, key_owner = jax.random.split(base_key, 5)
    groups = DEVICES // 4
    spare_blocks = 4 * OWNED - LIST_MAX
    first_share = jax.random.randint(key_first, (groups,), 0, spare_blocks + 1)
    second_share = jax.random.randint(key_second, (groups,), 0, 1 << 20) % (spare_blocks - first_share + 1)
    third_share = spare_blocks - first_share - second_share
    pattern = jnp.stack([jnp.full((groups,), LIST_MAX, jnp.int32), first_share, second_share, third_share], axis=1).reshape(-1).astype(jnp.int32)
    placing = jax.random.permutation(key_place, DEVICES)
    counts = jnp.zeros((DEVICES,), jnp.int32).at[placing].set(pattern)
    block_count = CX * CY
    scores = jax.random.randint(key_blocks, (DEVICES, block_count), 0, 1 << 20) * block_count + jnp.arange(block_count, dtype=jnp.int32)[None, :]
    chosen = jnp.argsort(scores, axis=1)[:, :LIST_MAX].astype(jnp.int32)
    positions = jnp.arange(LIST_MAX, dtype=jnp.int32)[None, :]
    present = positions < counts[:, None]
    starting = jnp.cumsum(counts) - counts
    serial = starting[:, None] + positions
    owners = jax.random.permutation(key_owner, DEVICES).astype(jnp.int32)[serial % DEVICES]
    return (jnp.where(present, chosen, -1).astype(jnp.int32), jnp.where(present, owners, -1).astype(jnp.int32))


def draw_react_list(key, part):
    return layout(key)[0]


def draw_owner_table(key, part):
    return layout(key)[1]


def shard_levels(rng, dims, shards, least, high):
    factor_of = 1.0
    for dim, parts in shards:
        heights = jax.random.uniform(jax.random.fold_in(jax.random.fold_in(rng, 6), dim), (parts,), jnp.float32, least / len(shards), high / len(shards))
        factor_of = factor_of * jnp.repeat(jnp.exp(heights), dims[dim] // parts).reshape((-1,) + (1,) * (len(dims) - 1 - dim))
    return factor_of


def bell_draw(stream_key, extent, deviation, reach, held_as=jnp.bfloat16):
    return jnp.clip(deviation * jax.random.normal(stream_key, extent, jnp.float32), -reach, reach).astype(held_as)


def setup_inputs(seed: int = 0) -> dict:
    key_list = jax.random.split(jax.random.key(seed), 14)
    fields = draw_fields(jax.random.fold_in(key_list[13], 71), 0)
    velocity = jnp.clip(jax.random.uniform(key_list[1], (3, NX, NY, NZ), jnp.float32, -0.4, 0.4) * shard_levels(key_list[1], (3, NX, NY, NZ), ((1, 4), (2, 4), (3, 2)), -0.4, 0.0), -0.4, 0.4)
    diffusivity = jnp.clip(jnp.exp(jax.random.uniform(key_list[2], (FIELDS,), jnp.float32, math.log(0.02), math.log(0.15))), 0.02, 0.15)
    weight_in = bell_draw(key_list[3], (FIELDS, HID_ONE), FIELDS ** -0.5, 1.25)
    bias_in = bell_draw(key_list[4], (HID_ONE,), 0.5, 3.0, jnp.float32)
    weight_mid = bell_draw(key_list[5], (HID_ONE, HID_TWO), HID_ONE ** -0.5, 0.15625)
    bias_mid = bell_draw(key_list[6], (HID_TWO,), 0.5, 3.0, jnp.float32)
    weight_low = bell_draw(key_list[7], (HID_TWO, HID_THREE), HID_TWO ** -0.5, 0.21875)
    bias_low = bell_draw(key_list[8], (HID_THREE,), 0.5, 3.0, jnp.float32)
    weight_out = bell_draw(key_list[9], (HID_THREE, FIELDS), HID_THREE ** -0.5, 0.3125)
    bias_out = bell_draw(key_list[10], (FIELDS,), 0.5, 3.0, jnp.float32)
    react_list = draw_react_list(jax.random.fold_in(key_list[13], 71), 0)
    owner_table = draw_owner_table(jax.random.fold_in(key_list[13], 71), 0)
    return {"fields": fields, "velocity": velocity, "diffusivity": diffusivity, "weight_in": weight_in, "bias_in": bias_in, "weight_mid": weight_mid, "bias_mid": bias_mid, "weight_low": weight_low, "bias_low": bias_low, "weight_out": weight_out, "bias_out": bias_out, "react_list": react_list, "owner_table": owner_table}


viscous = 0.05
third_part = 1.0 / 3.0


def laplace(values_in):
    summed = -6.0 * values_in
    for axis_dim in (1, 2, 3):
        summed = summed + jnp.roll(values_in, -1, axis_dim) + jnp.roll(values_in, 1, axis_dim)
    return summed


def transport(values_in, speeds):
    spread = -6.0 * values_in
    flux_sum = jnp.zeros_like(values_in)
    for axis_dim in (1, 2, 3):
        carried = speeds[axis_dim - 1][None] * values_in
        flux_sum = flux_sum + 0.5 * (jnp.roll(carried, -1, axis_dim) - jnp.roll(carried, 1, axis_dim))
        spread = spread + jnp.roll(values_in, -1, axis_dim) + jnp.roll(values_in, 1, axis_dim)
    return viscous * spread - flux_sum


def network(cell_rows, weight_in, bias_in, weight_mid, bias_mid, weight_low, bias_low, weight_out, bias_out):
    hidden = jax.nn.silu(jnp.dot(cell_rows, weight_in, preferred_element_type=jnp.float32) + bias_in).astype(jnp.bfloat16)
    hidden = jax.nn.silu(jnp.dot(hidden, weight_mid, preferred_element_type=jnp.float32) + bias_mid).astype(jnp.bfloat16)
    hidden = jax.nn.silu(jnp.dot(hidden, weight_low, preferred_element_type=jnp.float32) + bias_low).astype(jnp.bfloat16)
    return jnp.dot(hidden, weight_out, preferred_element_type=jnp.float32) + bias_out


def reference(fields, velocity, diffusivity, weight_in, bias_in, weight_mid, bias_mid, weight_low, bias_low, weight_out, bias_out, react_list, owner_table):
    section_one = fields + transport(fields, velocity)
    section_two = 0.75 * fields + 0.25 * (section_one + transport(section_one, velocity))
    flowed = third_part * fields + (2.0 / 3.0) * (section_two + transport(section_two, velocity))

    devices = N_GX * N_GY * N_GZ
    device = jnp.arange(devices, dtype=jnp.int32)[:, None]
    brick_x = device // (N_GY * N_GZ)
    brick_y = (device // N_GZ) % N_GY
    brick_z = device % N_GZ
    present = react_list >= 0
    clipped = jnp.where(present, react_list, 0).astype(jnp.int32)
    column_x = (brick_x * CX + clipped // CY).reshape(-1).astype(jnp.int32)
    column_y = (brick_y * CY + clipped % CY).reshape(-1).astype(jnp.int32)
    column_z = jnp.broadcast_to(brick_z * CZ, react_list.shape).reshape(-1).astype(jnp.int32)
    ordering = jnp.argsort(jnp.where(present, 0, 1).reshape(-1).astype(jnp.int32), stable=True)[: devices * OWNED]
    column_x = column_x[ordering]
    column_y = column_y[ordering]
    column_z = column_z[ordering]
    owners = owner_table.reshape(-1)[ordering].astype(jnp.int32)

    def fetch_block(start_x, start_y, start_z):
        piece = lax.dynamic_slice(flowed, (jnp.int32(0), start_x, start_y, start_z), (FIELDS, 1, 1, CZ))
        return piece.reshape(FIELDS, CZ)

    blocks = jax.vmap(fetch_block)(column_x, column_y, column_z)
    cell_rows = blocks.astype(jnp.bfloat16).transpose(0, 2, 1).reshape(devices, OWNED * CZ, FIELDS)

    def run_owner(portion):
        return network(portion, weight_in, bias_in, weight_mid, bias_mid, weight_low, bias_low, weight_out, bias_out)

    increments = lax.map(run_owner, cell_rows)
    increments = increments.reshape(devices * OWNED, CZ, FIELDS).transpose(0, 2, 1)
    block_heat = jnp.mean(increments[:, 0, :] ** 2, axis=-1)
    owner_activity = jax.ops.segment_sum(block_heat, owners, num_segments=devices) / 8.0

    offsets = column_z[:, None] + jnp.arange(CZ, dtype=jnp.int32)[None, :]
    reacted = flowed.at[:, column_x[:, None], column_y[:, None], offsets].add(increments.transpose(1, 0, 2))
    updated = reacted + diffusivity[:, None, None, None] * laplace(reacted)
    return updated, owner_activity
```

```python
import functools

import jax
import jax.numpy as jnp
from jax import lax
from jax.experimental import pallas as pl
from jax.experimental.pallas import tpu as pltpu
from jax.sharding import PartitionSpec as P

AXES = ("gx", "gy", "gz")
MESH = pl.DeviceIdType.MESH
SUB = 8
LANES = 128
VMEM_LIMIT = 60 * 1024 * 1024


def neighbours():
    ids = {a: lax.axis_index(a) for a in AXES}
    out = []
    for a in AXES:
        n = lax.axis_size(a)
        up = dict(ids)
        up[a] = lax.rem(ids[a] + 1, n)
        down = dict(ids)
        down[a] = lax.rem(ids[a] + n - 1, n)
        out.append((tuple(up[b] for b in AXES), tuple(down[b] for b in AXES)))
    return out


def enter(near):
    barrier = pltpu.get_barrier_semaphore()
    for up, down in near:
        pl.semaphore_signal(barrier, inc=1, device_id=up, device_id_type=MESH)
        pl.semaphore_signal(barrier, inc=1, device_id=down, device_id_type=MESH)
    pl.semaphore_wait(barrier, 6)


class Halo:
    def __init__(self, near, cx, cy, xs, xr, yr, zs, zr, send_sem, recv_sem):
        self.near, self.cx, self.cy = near, cx, cy
        self.xs, self.xr, self.yr, self.zs, self.zr = xs, xr, yr, zs, zr
        self.send_sem, self.recv_sem = send_sem, recv_sem

    def copies(self, slot, u):
        cx, cy = self.cx, self.cy
        (xu, xd), (yu, yd), (zu, zd) = self.near
        plan = [
            (self.xs.at[slot, 1], self.xr.at[slot, 0], xu),
            (self.xs.at[slot, 0], self.xr.at[slot, 1], xd),
            (u.at[pl.ds(1, cx), cy], self.yr.at[slot, 0], yu),
            (u.at[pl.ds(1, cx), 1], self.yr.at[slot, 1], yd),
            (self.zs.at[slot, 1], self.zr.at[slot, 0], zu),
            (self.zs.at[slot, 0], self.zr.at[slot, 1], zd),
        ]
        return [
            pltpu.make_async_remote_copy(
                src_ref=s, dst_ref=d, send_sem=self.send_sem.at[slot, i],
                recv_sem=self.recv_sem.at[slot, i], device_id=to, device_id_type=MESH)
            for i, (s, d, to) in enumerate(plan)
        ]

    def send(self, slot, u):
        for side, x in ((0, 1), (1, self.cx)):
            for k in range(self.cy // 2):
                pair = jnp.concatenate([u[x, 1 + 2 * k], u[x, 2 + 2 * k]], axis=0)
                self.xs[slot, side, k] = pair.astype(jnp.bfloat16)
        for c in self.copies(slot, u):
            c.start()

    def receive(self, slot, u):
        for c in self.copies(slot, u):
            c.wait_recv()
        for side, x in ((0, 0), (1, self.cx + 1)):
            for k in range(self.cy // 2):
                pair = self.xr[slot, side, k].astype(jnp.float32)
                u[x, 1 + 2 * k] = pair[:SUB]
                u[x, 2 + 2 * k] = pair[SUB:]
        for side, y in ((0, 0), (1, self.cy + 1)):
            for x in range(self.cx):
                u[1 + x, y] = self.yr[slot, side, x]

    def finish(self, slot, u):
        for c in self.copies(slot, u):
            c.wait_send()


def lane_ids():
    return lax.broadcasted_iota(jnp.int32, (SUB, LANES), 1)


def face_add(lane, y, t, low, high):
    low = jnp.where(lane == y, pltpu.roll(t, y, 1) if y else t, low)
    high = jnp.where(lane == y, pltpu.roll(t, y + 1, 1), high)
    return low, high


def z_near(lane, y, t, zr_low, zr_high):
    last = pltpu.roll(zr_high, LANES - 1 - y, 1)
    first = pltpu.roll(zr_low, LANES - y, 1) if y else zr_low
    after = jnp.where(lane == LANES - 1, last, pltpu.roll(t, LANES - 1, 1))
    before = jnp.where(lane == 0, first, pltpu.roll(t, 1, 1))
    return after, before


def load_chunk(halo, slot, src, u):
    lane = lane_ids()

    def body(x, _):
        low = jnp.zeros((SUB, LANES), jnp.float32)
        high = low
        for y in range(halo.cy):
            t = src[x, y]
            u[1 + x, 1 + y] = t
            low, high = face_add(lane, y, t, low, high)
        halo.zs[slot, 0, x] = low
        halo.zs[slot, 1, x] = high
        return 0

    lax.fori_loop(0, halo.cx, body, 0)


def flow_kernel(chunks, cx, cy, q_ref, v_ref, out_ref, u_ref, w_ref, coef,
                xs, xr, yr, zs, zr, send_sem, recv_sem):
    near = neighbours()
    enter(near)
    halo = Halo(near, cx, cy, xs, xr, yr, zs, zr, send_sem, recv_sem)
    lane = lane_ids()
    v_slot = 3 * chunks
    load_chunk(halo, v_slot, v_ref, w_ref)
    halo.send(v_slot, w_ref)
    for c in range(chunks):
        load_chunk(halo, c, q_ref.at[c], u_ref.at[0, c])
        halo.send(c, u_ref.at[0, c])
    halo.receive(v_slot, w_ref)

    def make_coef(x, _):
        zl, zh = zr[v_slot, 0, x], zr[v_slot, 1, x]
        for y in range(cy):
            t = w_ref[1 + x, 1 + y]
            za, zb = z_near(lane, y, t, zl, zh)
            rows = (
                0.05 - 0.5 * w_ref[2 + x, 1 + y][0:1],
                0.05 + 0.5 * w_ref[x, 1 + y][0:1],
                0.05 - 0.5 * w_ref[1 + x, 2 + y][1:2],
                0.05 + 0.5 * w_ref[1 + x, y][1:2],
                0.05 - 0.5 * za[2:3],
                0.05 + 0.5 * zb[2:3],
            )
            for i, r in enumerate(rows):
                coef[i, x, y] = jnp.broadcast_to(r, (SUB, LANES))
        return 0

    lax.fori_loop(0, cx, make_coef, 0)

    for stage in range(3):
        weight = (1.0 / 3.0, 0.5, 1.0)[stage]
        for c in range(chunks):
            slot = stage * chunks + c
            u = u_ref.at[stage, c]
            halo.receive(slot, u)

            def body(x, _):
                zl, zh = zr[slot, 0, x], zr[slot, 1, x]
                low = jnp.zeros((SUB, LANES), jnp.float32)
                high = low
                for y in range(cy):
                    t = u[1 + x, 1 + y]
                    za, zb = z_near(lane, y, t, zl, zh)
                    s = coef[0, x, y] * u[2 + x, 1 + y] + coef[1, x, y] * u[x, 1 + y]
                    s = s + (coef[2, x, y] * u[1 + x, 2 + y] + coef[3, x, y] * u[1 + x, y])
                    s = s + (coef[4, x, y] * za + coef[5, x, y] * zb)
                    r = q_ref[c, x, y] + weight * (s - 0.3 * t)
                    if stage == 2:
                        out_ref[c, x, y] = r
                    else:
                        u_ref[stage + 1, c, 1 + x, 1 + y] = r
                        low, high = face_add(lane, y, r, low, high)
                if stage < 2:
                    zs[slot + chunks, 0, x] = low
                    zs[slot + chunks, 1, x] = high
                return 0

            lax.fori_loop(0, cx, body, 0)
            if stage < 2:
                halo.send(slot + chunks, u_ref.at[stage + 1, c])
    for stage in range(3):
        for c in range(chunks):
            halo.finish(stage * chunks + c, u_ref.at[stage, c])
    halo.finish(v_slot, w_ref)


def diffuse_kernel(chunks, cx, cy, q_ref, d_ref, out_ref, u_ref,
                   xs, xr, yr, zs, zr, send_sem, recv_sem):
    near = neighbours()
    enter(near)
    halo = Halo(near, cx, cy, xs, xr, yr, zs, zr, send_sem, recv_sem)
    lane = lane_ids()
    for c in range(chunks):
        load_chunk(halo, c, q_ref.at[c], u_ref.at[c])
        halo.send(c, u_ref.at[c])
    for c in range(chunks):
        u = u_ref.at[c]
        halo.receive(c, u)
        rate = d_ref[c]

        def body(x, _):
            zl, zh = zr[c, 0, x], zr[c, 1, x]
            for y in range(cy):
                t = u[1 + x, 1 + y]
                za, zb = z_near(lane, y, t, zl, zh)
                s = (u[2 + x, 1 + y] + u[x, 1 + y]) + (u[1 + x, 2 + y] + u[1 + x, y])
                s = s + (za + zb)
                out_ref[c, x, y] = t + rate * (s - 6.0 * t)
            return 0

        lax.fori_loop(0, cx, body, 0)
    for c in range(chunks):
        halo.finish(c, u_ref.at[c])


def chem_kernel(chunks, cy, group, list_ref, owner_ref, q_ref, w1, w2, w3, w4,
                out_ref, act_ref, x_in, h1, h2, h3, inc):
    listed = list_ref.shape[0]
    n_lanes = group * LANES
    out_ref[...] = q_ref[...]
    act_ref[...] = jnp.zeros_like(act_ref)
    flat = (lax.broadcasted_iota(jnp.int32, (SUB, LANES), 0) * LANES + lane_ids())
    row = lax.broadcasted_iota(jnp.int32, (16, n_lanes), 0)
    ones = jnp.where(row < 3, 1.0, 0.0)
    fields = chunks * SUB
    x_in[fields:fields + SUB] = ones[:SUB]
    for h in (h1, h2, h3):
        h[h.shape[0] - 16:] = ones.astype(jnp.bfloat16)
    count = lax.fori_loop(
        0, listed, lambda i, n: n + jnp.where(list_ref[i] >= 0, 1, 0), 0)

    def layer(w, src, dst, step):
        rows = w.shape[0]
        for m in range(0, rows, step):
            k = min(step, rows - m)
            h = jnp.dot(w[m:m + k], src, preferred_element_type=jnp.float32)
            dst[m:m + k] = (h + h * jnp.tanh(h)).astype(jnp.bfloat16)

    def run(g, _):
        base = g * group
        for i in range(group):
            b = jnp.maximum(list_ref[base + i], 0)
            x, y = b // cy, lax.rem(b, cy)
            for c in range(chunks):
                x_in[c * SUB:(c + 1) * SUB, i * LANES:(i + 1) * LANES] = q_ref[c, x, y]
        layer(w1, x_in[...].astype(jnp.bfloat16), h1, 400)
        layer(w2, h1[...], h2, 400)
        layer(w3, h2[...], h3, 400)
        inc[...] = jnp.dot(w4[...], h3[...], preferred_element_type=jnp.float32)
        for i in range(group):
            entry = list_ref[base + i]
            b = jnp.maximum(entry, 0)
            valid = jnp.where(entry >= 0, 1.0, 0.0)
            x, y = b // cy, lax.rem(b, cy)
            for c in range(chunks):
                t = inc[c * SUB:(c + 1) * SUB, i * LANES:(i + 1) * LANES]
                out_ref[c, x, y] = out_ref[c, x, y] + valid * t
            r = inc[0:1, i * LANES:(i + 1) * LANES]
            heat = jnp.sum(r * r, axis=1, keepdims=True) * (valid / (8.0 * LANES))
            act_ref[...] = act_ref[...] + jnp.where(flat == owner_ref[base + i], heat, 0.0)
        return 0

    lax.fori_loop(0, (count + group - 1) // group, run, 0)


def bias_columns(bias, scale):
    rest = bias * scale
    columns = []
    for _ in range(3):
        part = lax.reduce_precision(rest, 8, 7)
        rest = rest - part
        columns.append(part)
    columns = jnp.stack(columns, axis=1).astype(jnp.bfloat16)
    return columns


def folded(weight, bias, scale, pad):
    cols = bias_columns(bias, scale)
    cols = jnp.pad(cols, ((0, 0), (0, pad - 3)))
    return jnp.concatenate([weight.T * jnp.bfloat16(scale), cols], axis=1)


def vmem(n):
    return [pl.BlockSpec(memory_space=pltpu.VMEM)] * n


def halo_scratch(slots, cx, cy):
    return [
        pltpu.VMEM((slots, 2, cy // 2, 2 * SUB, LANES), jnp.bfloat16),
        pltpu.VMEM((slots, 2, cy // 2, 2 * SUB, LANES), jnp.bfloat16),
        pltpu.VMEM((slots, 2, cx, SUB, LANES), jnp.float32),
        pltpu.VMEM((slots, 2, cx, SUB, LANES), jnp.float32),
        pltpu.VMEM((slots, 2, cx, SUB, LANES), jnp.float32),
        pltpu.SemaphoreType.DMA((slots, 6)),
        pltpu.SemaphoreType.DMA((slots, 6)),
    ]


def local(fields, velocity, diffusivity, weight_in, bias_in, weight_mid, bias_mid,
          weight_low, bias_low, weight_out, bias_out, react_list, owner_table):
    nf, cx, cy, cz = fields.shape
    chunks = nf // SUB
    shape = (chunks, cx, cy, SUB, cz)
    q = fields.reshape(chunks, SUB, cx, cy, cz).transpose(0, 2, 3, 1, 4)
    v = jnp.pad(velocity, ((0, SUB - 3), (0, 0), (0, 0), (0, 0))).transpose(1, 2, 0, 3)
    padded = (cx + 2, cy + 2, SUB, cz)
    slots = 3 * chunks + 1
    flowed = pl.pallas_call(
        functools.partial(flow_kernel, chunks, cx, cy),
        out_shape=jax.ShapeDtypeStruct(shape, jnp.float32),
        in_specs=vmem(2),
        out_specs=vmem(1)[0],
        scratch_shapes=[
            pltpu.VMEM((3, chunks) + padded, jnp.float32),
            pltpu.VMEM(padded, jnp.float32),
            pltpu.VMEM((6, cx, cy, SUB, cz), jnp.float32),
        ] + halo_scratch(slots, cx, cy),
        compiler_params=pltpu.CompilerParams(
            collective_id=0, has_side_effects=True, vmem_limit_bytes=VMEM_LIMIT),
        name="flow",
    )(q, v)

    listed = react_list.shape[1]
    group = 4
    h = (weight_in.shape[1], weight_mid.shape[1], weight_low.shape[1])
    w1 = folded(weight_in, bias_in, 0.5, SUB)
    w2 = folded(weight_mid, bias_mid, 0.5, 16)
    w3 = folded(weight_low, bias_low, 0.5, 16)
    w4 = folded(weight_out, bias_out, 1.0, 16)
    smem = pl.BlockSpec(memory_space=pltpu.SMEM)
    n_lanes = group * LANES
    reacted, activity = pl.pallas_call(
        functools.partial(chem_kernel, chunks, cy, group),
        out_shape=(jax.ShapeDtypeStruct(shape, jnp.float32),
                   jax.ShapeDtypeStruct((SUB, LANES), jnp.float32)),
        in_specs=[smem, smem] + vmem(5),
        out_specs=tuple(vmem(2)),
        scratch_shapes=[
            pltpu.VMEM((nf + SUB, n_lanes), jnp.float32),
            pltpu.VMEM((h[0] + 16, n_lanes), jnp.bfloat16),
            pltpu.VMEM((h[1] + 16, n_lanes), jnp.bfloat16),
            pltpu.VMEM((h[2] + 16, n_lanes), jnp.bfloat16),
            pltpu.VMEM((nf, n_lanes), jnp.float32),
        ],
        compiler_params=pltpu.CompilerParams(vmem_limit_bytes=VMEM_LIMIT),
        name="chem",
    )(react_list[0], owner_table[0], flowed, w1, w2, w3, w4)

    devices = lax.axis_size(AXES)
    mine = activity.reshape(-1)[:devices]
    owner_activity = jnp.sum(
        lax.all_to_all(mine, AXES, split_axis=0, concat_axis=0, tiled=True)).reshape(1)

    rates = jnp.broadcast_to(diffusivity.reshape(chunks, SUB, 1), (chunks, SUB, cz))
    updated = pl.pallas_call(
        functools.partial(diffuse_kernel, chunks, cx, cy),
        out_shape=jax.ShapeDtypeStruct(shape, jnp.float32),
        in_specs=vmem(2),
        out_specs=vmem(1)[0],
        scratch_shapes=[pltpu.VMEM((chunks,) + padded, jnp.float32)]
        + halo_scratch(chunks, cx, cy),
        compiler_params=pltpu.CompilerParams(
            collective_id=1, has_side_effects=True, vmem_limit_bytes=VMEM_LIMIT),
        name="diffuse",
    )(reacted, rates)
    updated = updated.transpose(0, 3, 1, 2, 4).reshape(nf, cx, cy, cz)
    return (updated, owner_activity)


def solution(mesh):
    return jax.shard_map(
        local,
        mesh=mesh,
        in_specs=(P(None, *AXES), P(None, *AXES)) + (P(),) * 9
        + (P(AXES, None), P(AXES, None)),
        out_specs=(P(None, *AXES), P(AXES)),
        check_vma=False,
    )
```

```python
import functools

import jax
import jax.numpy as jnp
from jax import lax
from jax.experimental import pallas as pl
from jax.experimental.pallas import tpu as pltpu
from jax.sharding import PartitionSpec as P

AXES = ("gx", "gy", "gz")
MESH = pl.DeviceIdType.MESH
SUB = 8
LANES = 128
VMEM_LIMIT = 60 * 1024 * 1024


def neighbours():
    ids = {a: lax.axis_index(a) for a in AXES}
    out = []
    for a in AXES:
        n = lax.axis_size(a)
        up = dict(ids)
        up[a] = lax.rem(ids[a] + 1, n)
        down = dict(ids)
        down[a] = lax.rem(ids[a] + n - 1, n)
        out.append((tuple(up[b] for b in AXES), tuple(down[b] for b in AXES)))
    return out


def enter(targets):
    barrier = pltpu.get_barrier_semaphore()
    for to in targets:
        pl.semaphore_signal(barrier, inc=1, device_id=to, device_id_type=MESH)
    pl.semaphore_wait(barrier, len(targets))


def peers(axis):
    ids = {a: lax.axis_index(a) for a in AXES}
    n = lax.axis_size(axis)
    out = []
    for k in range(1, n):
        to = dict(ids)
        to[axis] = lax.rem(ids[axis] + k, n)
        out.append(tuple(to[b] for b in AXES))
    return out


class Halo:
    def __init__(self, near, cx, cy, xs, xr, yr, zs, zr, send_sem, recv_sem):
        self.near, self.cx, self.cy = near, cx, cy
        self.xs, self.xr, self.yr, self.zs, self.zr = xs, xr, yr, zs, zr
        self.send_sem, self.recv_sem = send_sem, recv_sem

    def copies(self, slot, u):
        cx, cy = self.cx, self.cy
        (xu, xd), (yu, yd), (zu, zd) = self.near
        plan = [
            (self.xs.at[slot, 1], self.xr.at[slot, 0], xu),
            (self.xs.at[slot, 0], self.xr.at[slot, 1], xd),
            (u.at[pl.ds(1, cx), cy], self.yr.at[slot, 0], yu),
            (u.at[pl.ds(1, cx), 1], self.yr.at[slot, 1], yd),
            (self.zs.at[slot, 1], self.zr.at[slot, 0], zu),
            (self.zs.at[slot, 0], self.zr.at[slot, 1], zd),
        ]
        return [
            pltpu.make_async_remote_copy(
                src_ref=s, dst_ref=d, send_sem=self.send_sem.at[slot, i],
                recv_sem=self.recv_sem.at[slot, i], device_id=to, device_id_type=MESH)
            for i, (s, d, to) in enumerate(plan)
        ]

    def send(self, slot, u):
        for side, x in ((0, 1), (1, self.cx)):
            for k in range(self.cy // 2):
                pair = jnp.concatenate([u[x, 1 + 2 * k], u[x, 2 + 2 * k]], axis=0)
                self.xs[slot, side, k] = pair.astype(jnp.bfloat16)
        for c in self.copies(slot, u):
            c.start()

    def receive(self, slot, u):
        for c in self.copies(slot, u):
            c.wait_recv()
        for side, x in ((0, 0), (1, self.cx + 1)):
            for k in range(self.cy // 2):
                pair = self.xr[slot, side, k].astype(jnp.float32)
                u[x, 1 + 2 * k] = pair[:SUB]
                u[x, 2 + 2 * k] = pair[SUB:]
        for side, y in ((0, 0), (1, self.cy + 1)):
            for x in range(self.cx):
                u[1 + x, y] = self.yr[slot, side, x]

    def finish(self, slot, u):
        for c in self.copies(slot, u):
            c.wait_send()


def lane_ids():
    return lax.broadcasted_iota(jnp.int32, (SUB, LANES), 1)


def face_add(lane, y, t, low, high):
    low = jnp.where(lane == y, pltpu.roll(t, y, 1) if y else t, low)
    high = jnp.where(lane == y, pltpu.roll(t, y + 1, 1), high)
    return low, high


def z_near(lane, y, t, zr_low, zr_high):
    last = pltpu.roll(zr_high, LANES - 1 - y, 1)
    first = pltpu.roll(zr_low, LANES - y, 1) if y else zr_low
    after = jnp.where(lane == LANES - 1, last, pltpu.roll(t, LANES - 1, 1))
    before = jnp.where(lane == 0, first, pltpu.roll(t, 1, 1))
    return after, before


def load_chunk(halo, slot, src, u):
    lane = lane_ids()

    def body(x, _):
        low = jnp.zeros((SUB, LANES), jnp.float32)
        high = low
        for y in range(halo.cy):
            t = src[x, y]
            u[1 + x, 1 + y] = t
            low, high = face_add(lane, y, t, low, high)
        halo.zs[slot, 0, x] = low
        halo.zs[slot, 1, x] = high
        return 0

    lax.fori_loop(0, halo.cx, body, 0)


def flow_kernel(chunks, cx, cy, q_ref, v_ref, out_ref, u_ref, w_ref, coef,
                xs, xr, yr, zs, zr, send_sem, recv_sem):
    near = neighbours()
    enter([to for pair in near for to in pair])
    halo = Halo(near, cx, cy, xs, xr, yr, zs, zr, send_sem, recv_sem)
    lane = lane_ids()
    v_slot = 3 * chunks
    load_chunk(halo, v_slot, v_ref, w_ref)
    halo.send(v_slot, w_ref)
    for c in range(chunks):
        load_chunk(halo, c, q_ref.at[c], u_ref.at[0, c])
        halo.send(c, u_ref.at[0, c])
    halo.receive(v_slot, w_ref)

    def make_coef(x, _):
        zl, zh = zr[v_slot, 0, x], zr[v_slot, 1, x]
        for y in range(cy):
            t = w_ref[1 + x, 1 + y]
            za, zb = z_near(lane, y, t, zl, zh)
            rows = (
                0.05 - 0.5 * w_ref[2 + x, 1 + y][0:1],
                0.05 + 0.5 * w_ref[x, 1 + y][0:1],
                0.05 - 0.5 * w_ref[1 + x, 2 + y][1:2],
                0.05 + 0.5 * w_ref[1 + x, y][1:2],
                0.05 - 0.5 * za[2:3],
                0.05 + 0.5 * zb[2:3],
            )
            for i, r in enumerate(rows):
                coef[i, x, y] = jnp.broadcast_to(r, (SUB, LANES))
        return 0

    lax.fori_loop(0, cx, make_coef, 0)

    for stage in range(3):
        weight = (1.0 / 3.0, 0.5, 1.0)[stage]
        for c in range(chunks):
            slot = stage * chunks + c
            u = u_ref.at[stage, c]
            halo.receive(slot, u)

            def body(x, _):
                zl, zh = zr[slot, 0, x], zr[slot, 1, x]
                low = jnp.zeros((SUB, LANES), jnp.float32)
                high = low
                for y in range(cy):
                    t = u[1 + x, 1 + y]
                    za, zb = z_near(lane, y, t, zl, zh)
                    s = coef[0, x, y] * u[2 + x, 1 + y] + coef[1, x, y] * u[x, 1 + y]
                    s = s + (coef[2, x, y] * u[1 + x, 2 + y] + coef[3, x, y] * u[1 + x, y])
                    s = s + (coef[4, x, y] * za + coef[5, x, y] * zb)
                    r = q_ref[c, x, y] + weight * (s - 0.3 * t)
                    if stage == 2:
                        out_ref[c, x, y] = r
                    else:
                        u_ref[stage + 1, c, 1 + x, 1 + y] = r
                        low, high = face_add(lane, y, r, low, high)
                if stage < 2:
                    zs[slot + chunks, 0, x] = low
                    zs[slot + chunks, 1, x] = high
                return 0

            lax.fori_loop(0, cx, body, 0)
            if stage < 2:
                halo.send(slot + chunks, u_ref.at[stage + 1, c])
    for stage in range(3):
        for c in range(chunks):
            halo.finish(stage * chunks + c, u_ref.at[stage, c])
    halo.finish(v_slot, w_ref)


def diffuse_kernel(chunks, cx, cy, q_ref, d_ref, act_in, out_ref, act_out, u_ref, part, got,
                   act_send, act_recv, xs, xr, yr, zs, zr, send_sem, recv_sem):
    near = neighbours()
    groups = [peers(a) for a in AXES[::-1]]
    enter([to for g in groups for to in g])
    halo = Halo(near, cx, cy, xs, xr, yr, zs, zr, send_sem, recv_sem)
    lane = lane_ids()

    def hops(phase):
        return [
            pltpu.make_async_remote_copy(
                src_ref=part.at[phase], dst_ref=got.at[phase, k],
                send_sem=act_send.at[phase, k], recv_sem=act_recv.at[phase, k],
                device_id=to, device_id_type=MESH)
            for k, to in enumerate(groups[phase])
        ]

    def gather(phase):
        for h in hops(phase):
            h.wait_recv()
        total = part[phase]
        for k in range(len(groups[phase])):
            total = total + got[phase, k]
        return total

    part[0] = act_in[...]
    for c in range(chunks):
        load_chunk(halo, c, q_ref.at[c], u_ref.at[c])
        halo.send(c, u_ref.at[c])
        if c == 0:
            for h in hops(0):
                h.start()
    for c in range(chunks):
        u = u_ref.at[c]
        if c < len(groups) - 1:
            part[c + 1] = gather(c)
            for h in hops(c + 1):
                h.start()
        halo.receive(c, u)
        rate = d_ref[c]

        def body(x, _):
            zl, zh = zr[c, 0, x], zr[c, 1, x]
            for y in range(cy):
                t = u[1 + x, 1 + y]
                za, zb = z_near(lane, y, t, zl, zh)
                s = (u[2 + x, 1 + y] + u[x, 1 + y]) + (u[1 + x, 2 + y] + u[1 + x, y])
                s = s + (za + zb)
                out_ref[c, x, y] = t + rate * (s - 6.0 * t)
            return 0

        lax.fori_loop(0, cx, body, 0)
    done = min(chunks, len(groups) - 1)
    for phase in range(done, len(groups) - 1):
        part[phase + 1] = gather(phase)
        for h in hops(phase + 1):
            h.start()
    total = gather(len(groups) - 1)
    me = (lax.axis_index("gx") * lax.axis_size("gy") + lax.axis_index("gy")) * lax.axis_size(
        "gz") + lax.axis_index("gz")
    flat = lax.broadcasted_iota(jnp.int32, (SUB, LANES), 0) * LANES + lane
    mine = jnp.where(flat == me, total, 0.0)
    act_out[...] = jnp.broadcast_to(
        jnp.sum(jnp.sum(mine, axis=1, keepdims=True), axis=0, keepdims=True), (SUB, LANES))
    for phase in range(len(groups)):
        for h in hops(phase):
            h.wait_send()
    for c in range(chunks):
        halo.finish(c, u_ref.at[c])


def chem_kernel(chunks, cy, group, list_ref, owner_ref, q_ref, w1, w2, w3, w4,
                out_ref, act_ref, x_in, h1, h2, h3, inc):
    listed = list_ref.shape[0]
    n_lanes = group * LANES
    out_ref[...] = q_ref[...]
    act_ref[...] = jnp.zeros_like(act_ref)
    flat = (lax.broadcasted_iota(jnp.int32, (SUB, LANES), 0) * LANES + lane_ids())
    row = lax.broadcasted_iota(jnp.int32, (16, n_lanes), 0)
    ones = jnp.where(row < 3, 1.0, 0.0)
    fields = chunks * SUB
    x_in[fields:fields + SUB] = ones[:SUB]
    for h in (h1, h2, h3):
        h[h.shape[0] - 16:] = ones.astype(jnp.bfloat16)
    count = lax.fori_loop(
        0, listed, lambda i, n: n + jnp.where(list_ref[i] >= 0, 1, 0), 0)

    def layer(w, src, dst, step):
        rows = w.shape[0]
        for m in range(0, rows, step):
            k = min(step, rows - m)
            h = jnp.dot(w[m:m + k], src, preferred_element_type=jnp.float32)
            dst[m:m + k] = (h + h * jnp.tanh(h)).astype(jnp.bfloat16)

    def run(g, _):
        base = g * group
        for i in range(group):
            b = jnp.maximum(list_ref[base + i], 0)
            x, y = b // cy, lax.rem(b, cy)
            for c in range(chunks):
                x_in[c * SUB:(c + 1) * SUB, i * LANES:(i + 1) * LANES] = q_ref[c, x, y]
        layer(w1, x_in[...].astype(jnp.bfloat16), h1, 400)
        layer(w2, h1[...], h2, 400)
        layer(w3, h2[...], h3, 400)
        inc[...] = jnp.dot(w4[...], h3[...], preferred_element_type=jnp.float32)
        for i in range(group):
            entry = list_ref[base + i]
            b = jnp.maximum(entry, 0)
            valid = jnp.where(entry >= 0, 1.0, 0.0)
            x, y = b // cy, lax.rem(b, cy)
            for c in range(chunks):
                t = inc[c * SUB:(c + 1) * SUB, i * LANES:(i + 1) * LANES]
                out_ref[c, x, y] = out_ref[c, x, y] + valid * t
            r = inc[0:1, i * LANES:(i + 1) * LANES]
            heat = jnp.sum(r * r, axis=1, keepdims=True) * (valid / (8.0 * LANES))
            act_ref[...] = act_ref[...] + jnp.where(flat == owner_ref[base + i], heat, 0.0)
        return 0

    lax.fori_loop(0, (count + group - 1) // group, run, 0)


def bias_columns(bias, scale):
    rest = bias * scale
    columns = []
    for _ in range(3):
        part = lax.reduce_precision(rest, 8, 7)
        rest = rest - part
        columns.append(part)
    columns = jnp.stack(columns, axis=1).astype(jnp.bfloat16)
    return columns


def folded(weight, bias, scale, pad):
    cols = bias_columns(bias, scale)
    cols = jnp.pad(cols, ((0, 0), (0, pad - 3)))
    return jnp.concatenate([weight.T * jnp.bfloat16(scale), cols], axis=1)


def vmem(n):
    return [pl.BlockSpec(memory_space=pltpu.VMEM)] * n


def halo_scratch(slots, cx, cy):
    return [
        pltpu.VMEM((slots, 2, cy // 2, 2 * SUB, LANES), jnp.bfloat16),
        pltpu.VMEM((slots, 2, cy // 2, 2 * SUB, LANES), jnp.bfloat16),
        pltpu.VMEM((slots, 2, cx, SUB, LANES), jnp.float32),
        pltpu.VMEM((slots, 2, cx, SUB, LANES), jnp.float32),
        pltpu.VMEM((slots, 2, cx, SUB, LANES), jnp.float32),
        pltpu.SemaphoreType.DMA((slots, 6)),
        pltpu.SemaphoreType.DMA((slots, 6)),
    ]


def local(fields, velocity, diffusivity, weight_in, bias_in, weight_mid, bias_mid,
          weight_low, bias_low, weight_out, bias_out, react_list, owner_table):
    nf, cx, cy, cz = fields.shape
    chunks = nf // SUB
    shape = (chunks, cx, cy, SUB, cz)
    q = fields.reshape(chunks, SUB, cx, cy, cz).transpose(0, 2, 3, 1, 4)
    v = jnp.pad(velocity, ((0, SUB - 3), (0, 0), (0, 0), (0, 0))).transpose(1, 2, 0, 3)
    padded = (cx + 2, cy + 2, SUB, cz)
    slots = 3 * chunks + 1
    flowed = pl.pallas_call(
        functools.partial(flow_kernel, chunks, cx, cy),
        out_shape=jax.ShapeDtypeStruct(shape, jnp.float32),
        in_specs=vmem(2),
        out_specs=vmem(1)[0],
        scratch_shapes=[
            pltpu.VMEM((3, chunks) + padded, jnp.float32),
            pltpu.VMEM(padded, jnp.float32),
            pltpu.VMEM((6, cx, cy, SUB, cz), jnp.float32),
        ] + halo_scratch(slots, cx, cy),
        compiler_params=pltpu.CompilerParams(
            collective_id=0, has_side_effects=True, vmem_limit_bytes=VMEM_LIMIT),
        name="flow",
    )(q, v)

    listed = react_list.shape[1]
    group = 4
    h = (weight_in.shape[1], weight_mid.shape[1], weight_low.shape[1])
    w1 = folded(weight_in, bias_in, 0.5, SUB)
    w2 = folded(weight_mid, bias_mid, 0.5, 16)
    w3 = folded(weight_low, bias_low, 0.5, 16)
    w4 = folded(weight_out, bias_out, 1.0, 16)
    smem = pl.BlockSpec(memory_space=pltpu.SMEM)
    n_lanes = group * LANES
    reacted, activity = pl.pallas_call(
        functools.partial(chem_kernel, chunks, cy, group),
        out_shape=(jax.ShapeDtypeStruct(shape, jnp.float32),
                   jax.ShapeDtypeStruct((SUB, LANES), jnp.float32)),
        in_specs=[smem, smem] + vmem(5),
        out_specs=tuple(vmem(2)),
        scratch_shapes=[
            pltpu.VMEM((nf + SUB, n_lanes), jnp.float32),
            pltpu.VMEM((h[0] + 16, n_lanes), jnp.bfloat16),
            pltpu.VMEM((h[1] + 16, n_lanes), jnp.bfloat16),
            pltpu.VMEM((h[2] + 16, n_lanes), jnp.bfloat16),
            pltpu.VMEM((nf, n_lanes), jnp.float32),
        ],
        compiler_params=pltpu.CompilerParams(vmem_limit_bytes=VMEM_LIMIT),
        name="chem",
    )(react_list[0], owner_table[0], flowed, w1, w2, w3, w4)

    rates = jnp.broadcast_to(diffusivity.reshape(chunks, SUB, 1), (chunks, SUB, cz))
    most = max(lax.axis_size(a) for a in AXES) - 1
    updated, mine = pl.pallas_call(
        functools.partial(diffuse_kernel, chunks, cx, cy),
        out_shape=(jax.ShapeDtypeStruct(shape, jnp.float32),
                   jax.ShapeDtypeStruct((SUB, LANES), jnp.float32)),
        in_specs=vmem(3),
        out_specs=tuple(vmem(2)),
        scratch_shapes=[
            pltpu.VMEM((chunks,) + padded, jnp.float32),
            pltpu.VMEM((len(AXES), SUB, LANES), jnp.float32),
            pltpu.VMEM((len(AXES), most, SUB, LANES), jnp.float32),
            pltpu.SemaphoreType.DMA((len(AXES), most)),
            pltpu.SemaphoreType.DMA((len(AXES), most)),
        ]
        + halo_scratch(chunks, cx, cy),
        compiler_params=pltpu.CompilerParams(
            collective_id=1, has_side_effects=True, vmem_limit_bytes=VMEM_LIMIT),
        name="diffuse",
    )(reacted, rates, activity)
    updated = updated.transpose(0, 3, 1, 2, 4).reshape(nf, cx, cy, cz)
    return (updated, mine[0, 0:1])


def solution(mesh):
    return jax.shard_map(
        local,
        mesh=mesh,
        in_specs=(P(None, *AXES), P(None, *AXES)) + (P(),) * 9
        + (P(AXES, None), P(AXES, None)),
        out_specs=(P(None, *AXES), P(AXES)),
        check_vma=False,
    )
```
